512 devices in a mesh: ctx: 128 (over y_hi, z, x), tp: 4 (over y_lo, core).
Axes of the slice: x: 4, y: 4 (y_hi: 2, y_lo: 2; y = y_hi * 2 + y_lo), z: 16, core: 2. Of those that a mesh axis runs over, the one named last changes fastest.
Arguments:
- residual: bfloat16 [32768, 8192], P('ctx', 'tp'), may hold values from -16 to 16
- features: bfloat16 [32768, 3, 8192], P('ctx', None, 'tp'), may hold values from -6 to 6
- short_taps: float32 [3, 3, 8192], P(None, None, 'tp'), may hold values from -3.5 to 3.5
- filter_taps: bfloat16 [512, 128], P('tp'), may hold values from -0.5 to 0.5
- skip_gain: float32 [8192], P('tp'), may hold values from -1 to 1
- norm_gain: float32 [8192], P('tp'), may hold values from 0.5 to 1.5
Outputs:
- normed: bfloat16 [32768, 8192], P('ctx', 'tp')
The draws below stay inside these ranges and needn't reach their ends.
All inputs are finite; a program needn't handle non-finite values.
Results may differ from the reference program's by a relative error of at most 0.0065.
Values may be sent and summed in bfloat16 or wider, within the bound.
No kernel may reach another device: no remote copies, remote signals or barrier semaphores. Data moves between devices by JAX's collectives and lax.ppermute only.
A program may use at most 128 MiB of HBM per device.

```python
import jax
import jax.numpy as jnp
from jax import lax

D = 8192
LF = 128
GROUPS = 512
TOKENS = 32768


def draw_residual(key, part):
    column = jnp.arange(D, dtype=jnp.float32) / D
    first_key = jax.random.fold_in(jax.random.fold_in(key, 11), 0)
    base_draw = jnp.clip(jax.random.normal(first_key, (TOKENS, D), jnp.float32), -6.0, 6.0)
    slopes = 0.5 + 1.5 * column
    return (base_draw * slopes).astype(jnp.bfloat16)


def levels(own_key, extent, shards, least, high):
    def one(dim, parts):
        heights = jax.random.uniform(jax.random.fold_in(jax.random.fold_in(own_key, 6), dim), (parts,), jnp.float32, least / len(shards), high / len(shards))
        return jnp.repeat(jnp.exp(heights), extent[dim] // parts).reshape((-1,) + (1,) * (len(extent) - dim - 1))

    gain = one(*shards[0])
    for cut in shards[1:]:
        gain = gain * one(*cut)
    return gain


def bell_draw(stream_key, extent, deviation, limit, pieces=(), kind=jnp.bfloat16):
    result = jax.random.normal(stream_key, extent, jnp.float32) * deviation
    if len(pieces) > 0:
        result = levels(stream_key, extent, pieces, -0.22, 0.18) * result
    return jnp.clip(result, min=-limit, max=limit).astype(kind)


def setup_inputs(seed: int = 0) -> dict:
    seeds = jax.random.split(jax.random.key(seed), 7)
    residual = draw_residual(jax.random.fold_in(seeds[6], 71), 0)
    features = bell_draw(seeds[1], (TOKENS, 3, D), 1.0, 6.0, ((0, 128), (2, 4)))
    short_taps = bell_draw(seeds[2], (3, 3, D), 3 ** -0.5, 3.5, ((2, 4),), jnp.float32)
    filter_taps = bell_draw(seeds[3], (GROUPS, LF), LF ** -0.5, 0.5, ((0, 4),))
    skip_gain = jnp.clip(jax.random.uniform(seeds[4], (D,), jnp.float32, -1.0, 1.0) * levels(seeds[4], (D,), ((0, 4),), -0.4, 0.0), -1.0, 1.0)
    norm_gain = jnp.clip(1.0 + 0.1 * jax.random.normal(seeds[5], (D,), jnp.float32), 0.5, 1.5)
    return dict(residual=residual, features=features, short_taps=short_taps, filter_taps=filter_taps, skip_gain=skip_gain, norm_gain=norm_gain)


def reference(residual, features, short_taps, filter_taps, skip_gain, norm_gain):
    group_size = D // GROUPS
    chan_block = min(D, 1024)
    num_blocks = D // chan_block
    taps_wide = jnp.repeat(filter_taps.astype(jnp.float32), group_size, axis=0)

    def one_block(block_index):
        offset_c = block_index * chan_block
        feat_in = lax.dynamic_slice_in_dim(features, offset_c, chan_block, 2).astype(jnp.float32)
        short_w = lax.dynamic_slice_in_dim(short_taps, offset_c, chan_block, 2)
        padded = jnp.concatenate([jnp.zeros((2, 3, chan_block), jnp.float32), feat_in], 0)
        featured = (short_w[0] * padded[2:] + short_w[1] * padded[1:-1] + short_w[2] * padded[:-2]).astype(jnp.bfloat16)
        gated_in = (featured[:, 1].astype(jnp.float32) * featured[:, 2].astype(jnp.float32)).astype(jnp.bfloat16)
        gated_f = gated_in.astype(jnp.float32)
        gated_pad = jnp.concatenate([jnp.zeros((LF - 1, chan_block), jnp.float32), gated_f], 0)
        taps_here = lax.dynamic_slice_in_dim(taps_wide, offset_c, chan_block, 0)

        def add_tap(tap_index, running):
            shifted = lax.dynamic_slice_in_dim(gated_pad, LF - 1 - tap_index, TOKENS, 0)
            tap_col = lax.dynamic_slice_in_dim(taps_here, tap_index, 1, 1)[:, 0]
            return running + tap_col * shifted
        filtered = lax.fori_loop(0, LF, add_tap, jnp.zeros((TOKENS, chan_block), jnp.float32))
        skip_here = lax.dynamic_slice_in_dim(skip_gain, offset_c, chan_block, 0)
        filtered = filtered + skip_here * gated_f
        resid_here = lax.dynamic_slice_in_dim(residual, offset_c, chan_block, 1).astype(jnp.float32)
        return (resid_here + featured[:, 0].astype(jnp.float32) * filtered).astype(jnp.bfloat16)
    streams = lax.map(one_block, jnp.arange(num_blocks, dtype=jnp.int32))
    stream = jnp.moveaxis(streams, 0, 1).reshape(TOKENS, D)
    stream_f = stream.astype(jnp.float32)
    mean_sq = lax.optimization_barrier(jnp.mean(stream_f * stream_f, axis=1, keepdims=True))
    return (stream_f * lax.rsqrt(mean_sq + 1e-06) * norm_gain).astype(jnp.bfloat16)
```

```python
import functools

import jax
import jax.numpy as jnp
from jax import lax
from jax.experimental import pallas as pl
from jax.experimental.pallas import tpu as pltpu
from jax.sharding import PartitionSpec as P

F32 = jnp.float32
BF16 = jnp.bfloat16
LANES = 128
HEAD = 80
TAIL = 48
EPS = 1e-06
HI = lax.Precision.HIGHEST
VMEM = pl.BlockSpec(memory_space=pltpu.VMEM)
MIB = 1 << 20


def causal3(x, w):
    return (w[0] * x + w[1] * pltpu.roll(x, 1, 0) + w[2] * pltpu.roll(x, 2, 0)).astype(BF16)


def tail_gate_kernel(kv_ref, q_ref, taps_ref, out_ref):
    halo = kv_ref.shape[1] - LANES
    key = kv_ref[0].astype(F32)
    val = kv_ref[1].astype(F32)
    k_feat = causal3(key, [taps_ref[s, 1:2] for s in range(3)])[halo:]
    v_feat = causal3(val, [taps_ref[s, 2:3] for s in range(3)])[halo:]
    out_ref[:LANES] = (k_feat.astype(F32) * v_feat.astype(F32)).astype(BF16)
    last_q = pltpu.roll(q_ref[0].astype(F32)[-8:], 2, 0)
    last_k = pltpu.roll(key[-8:], 4, 0)
    last_v = pltpu.roll(val[-8:], 6, 0)
    row = lax.broadcasted_iota(jnp.int32, last_q.shape, 0)
    rim = jnp.where(row < 2, last_q, jnp.where(row < 4, last_k, jnp.where(row < 6, last_v, 0.0)))
    out_ref[LANES:] = rim.astype(BF16)


def tail_gate(feats, short_taps):
    _, rows, channels = feats.shape
    width = channels // 4
    halo = 16
    return pl.pallas_call(
        tail_gate_kernel,
        grid=(channels // width,),
        in_specs=[
            pl.BlockSpec(
                (pl.Element(2), pl.Element(LANES + halo), pl.Element(width)),
                lambda i: (1, rows - LANES - halo, i * width),
            ),
            pl.BlockSpec(
                (pl.Element(1), pl.Element(16), pl.Element(width)),
                lambda i: (0, rows - 16, i * width),
            ),
            pl.BlockSpec((3, 3, width), lambda i: (0, 0, i)),
        ],
        out_specs=pl.BlockSpec((LANES + 8, width), lambda i: (0, i)),
        out_shape=jax.ShapeDtypeStruct((LANES + 8, channels), BF16),
        name="tail_gate",
    )(feats, feats, short_taps)


def group_select(prod, per_tile, rows):
    lane = lax.broadcasted_iota(jnp.int32, (rows, 2 * LANES), 1)
    owner = (lane % LANES) // (LANES // per_tile)
    acc = prod[:rows]
    for g in range(1, per_tile):
        acc = jnp.where(owner == g, prod[g * rows : (g + 1) * rows], acc)
    return jnp.concatenate([acc[:, :LANES], acc[:, LANES:]], 0)


def local_kernel(feats_ref, res_ref, short_ref, filt_ref, skip_ref, toep_ref, gate_ref, q_ref, stream_ref, ss_ref):
    tokens, channels = res_ref.shape
    tiles = channels // LANES
    per_tile = filt_ref.shape[0] // tiles
    first = tokens - 2 * TAIL
    tap = lax.broadcasted_iota(jnp.int32, (LANES, 2 * LANES), 0)
    pos = lax.broadcasted_iota(jnp.int32, (LANES, 2 * LANES), 1)
    flip = (tap + pos == LANES).astype(BF16)

    def tile(t, total):
        lanes = pl.ds(pl.multiple_of(t * LANES, LANES), LANES)
        feats = [
            causal3(feats_ref[s, :, lanes].astype(F32), [short_ref[i, s : s + 1, lanes] for i in range(3)])
            for s in range(3)
        ]
        gate = (feats[1].astype(F32) * feats[2].astype(F32)).astype(BF16)
        gate_ref[:, lanes] = gate
        q_ref[:, lanes] = feats[0]
        taps = filt_ref[pl.ds(pl.multiple_of(t * per_tile, per_tile), per_tile), :]
        base = jnp.dot(taps, flip, preferred_element_type=F32)
        lhs = []
        for g in range(per_tile):
            wide = jnp.broadcast_to(base[g : g + 1], (HEAD, 2 * LANES))
            band = pltpu.roll(wide, 0, 1, stride=1, stride_axis=0).astype(BF16)
            toep_ref[t, g * HEAD : (g + 1) * HEAD, :] = band
            lhs.append(band[:TAIL])
        z0 = jnp.zeros((first - LANES, LANES), BF16)
        z1 = jnp.zeros((first - LANES + TAIL, LANES), BF16)
        rhs = jnp.concatenate(
            [
                jnp.concatenate([gate[first - LANES :], z0], 0),
                jnp.concatenate([gate[first - LANES + TAIL :], z1], 0),
            ],
            1,
        )
        prod = jnp.dot(jnp.concatenate(lhs, 0), rhs, preferred_element_type=F32)
        filtered = group_select(prod, per_tile, TAIL)
        filtered = filtered + skip_ref[:, lanes] * gate[first:].astype(F32)
        stream = (res_ref[first:, lanes].astype(F32) + feats[0][first:].astype(F32) * filtered).astype(BF16)
        stream_ref[:, lanes] = stream
        wide_stream = stream.astype(F32)
        return total + wide_stream * wide_stream

    total = lax.fori_loop(0, tiles, tile, jnp.zeros((2 * TAIL, LANES), F32))
    ss_ref[...] = total


def local_part(feats, residual, short_taps, filter_taps, skip):
    _, tokens, channels = feats.shape
    tiles = channels // LANES
    per_tile = filter_taps.shape[0] // tiles
    return pl.pallas_call(
        local_kernel,
        in_specs=[VMEM] * 5,
        out_specs=[VMEM] * 5,
        out_shape=[
            jax.ShapeDtypeStruct((tiles, per_tile * HEAD, 2 * LANES), BF16),
            jax.ShapeDtypeStruct((tokens, channels), BF16),
            jax.ShapeDtypeStruct((tokens, channels), BF16),
            jax.ShapeDtypeStruct((2 * TAIL, channels), BF16),
            jax.ShapeDtypeStruct((2 * TAIL, LANES), F32),
        ],
        compiler_params=pltpu.CompilerParams(vmem_limit_bytes=48 * MIB),
        cost_estimate=pl.CostEstimate(flops=10**9, transcendentals=0, bytes_accessed=16 * MIB),
        name="local_part",
    )(feats, residual, short_taps, filter_taps, skip)


def head_kernel(carry_ref, feats_ref, res_ref, short_ref, skip_ref, toep_ref, gate_ref, q_ref, tail_ss_ref, stream_ref, ss_ref):
    channels = res_ref.shape[1]
    tiles = channels // LANES
    per_tile = toep_ref.shape[1] // HEAD
    rows = 2 * HEAD

    def tile(t, total):
        lanes = pl.ds(pl.multiple_of(t * LANES, LANES), LANES)
        rim = carry_ref[LANES:, lanes].astype(F32)
        row = lax.broadcasted_iota(jnp.int32, (16, LANES), 0)
        feats = []
        for s in range(3):
            x = feats_ref[s, :16, lanes].astype(F32)
            w = [short_ref[i, s : s + 1, lanes] for i in range(3)]
            older, newer = rim[2 * s : 2 * s + 1], rim[2 * s + 1 : 2 * s + 2]
            x1 = jnp.where(row == 0, newer, pltpu.roll(x, 1, 0))
            x2 = jnp.where(row == 0, older, jnp.where(row == 1, newer, pltpu.roll(x, 2, 0)))
            feats.append((w[0] * x + w[1] * x1 + w[2] * x2).astype(BF16))
        fixed = (feats[1].astype(F32) * feats[2].astype(F32)).astype(BF16)
        gate = jnp.concatenate([fixed, gate_ref[16 : 2 * LANES - LANES + HEAD, lanes]], 0)
        query = jnp.concatenate([feats[0], q_ref[16:rows, lanes]], 0)
        carry = carry_ref[:LANES, lanes]
        rhs = jnp.concatenate(
            [
                jnp.concatenate([carry, gate[:LANES]], 0),
                jnp.concatenate([carry[HEAD:], gate[: LANES + HEAD]], 0),
            ],
            1,
        )
        prod = jnp.dot(toep_ref[t], rhs, preferred_element_type=F32)
        filtered = group_select(prod, per_tile, HEAD)
        filtered = filtered + skip_ref[:, lanes] * gate[:rows].astype(F32)
        stream = (res_ref[:rows, lanes].astype(F32) + query.astype(F32) * filtered).astype(BF16)
        stream_ref[:, lanes] = stream
        wide_stream = stream.astype(F32)
        return total + wide_stream * wide_stream

    total = lax.fori_loop(0, tiles, tile, jnp.zeros((rows, LANES), F32))
    total = jnp.concatenate([total, tail_ss_ref[...]], 0)
    ones = jnp.ones((8, LANES), F32)
    ss_ref[...] = lax.dot_general(
        ones, total, (((1,), (1,)), ((), ())), precision=HI, preferred_element_type=F32
    )


def head_part(carry, feats, residual, short_taps, skip, toep, gate, query, tail_ss):
    tokens, channels = residual.shape
    return pl.pallas_call(
        head_kernel,
        in_specs=[VMEM] * 9,
        out_specs=[VMEM] * 2,
        out_shape=[
            jax.ShapeDtypeStruct((2 * HEAD, channels), BF16),
            jax.ShapeDtypeStruct((8, tokens), F32),
        ],
        compiler_params=pltpu.CompilerParams(vmem_limit_bytes=48 * MIB),
        name="head_part",
    )(carry, feats, residual, short_taps, skip, toep, gate, query, tail_ss)


def norm_kernel(width, ss_ref, head_ref, tail_ref, gain_ref, out_ref):
    ones = jnp.ones((ss_ref.shape[0], LANES), F32)
    sums = lax.dot_general(
        ss_ref[...], ones, (((0,), (0,)), ((), ())), precision=HI, preferred_element_type=F32
    )
    scale = lax.rsqrt(sums / width + EPS)
    split = head_ref.shape[0]
    for t in range(head_ref.shape[1] // LANES):
        lanes = slice(t * LANES, (t + 1) * LANES)
        out_ref[:split, lanes] = (head_ref[:, lanes].astype(F32) * scale[:split] * gain_ref[:, lanes]).astype(BF16)
        out_ref[split:, lanes] = (tail_ref[:, lanes].astype(F32) * scale[split:] * gain_ref[:, lanes]).astype(BF16)


def normalize(ss, head, tail, gain, width):
    tokens = head.shape[0] + tail.shape[0]
    channels = head.shape[1]
    return pl.pallas_call(
        functools.partial(norm_kernel, width),
        in_specs=[VMEM] * 4,
        out_specs=VMEM,
        out_shape=jax.ShapeDtypeStruct((tokens, channels), BF16),
        compiler_params=pltpu.CompilerParams(vmem_limit_bytes=48 * MIB),
        name="normalize",
    )(ss, head, tail, gain)


def on_device(residual, features, short_taps, filter_taps, skip_gain, norm_gain):
    channels = residual.shape[1]
    feats = jnp.transpose(features, (1, 0, 2))
    skip = skip_gain.reshape(1, channels)
    gain = norm_gain.reshape(1, channels)
    sent = tail_gate(feats, short_taps)
    size = lax.axis_size("ctx")
    carry = lax.ppermute(sent, "ctx", [(i, i + 1) for i in range(size - 1)])
    toep, gate, query, tail, tail_ss = local_part(feats, residual, short_taps, filter_taps, skip)
    head, ss = head_part(carry, feats, residual, short_taps, skip, toep, gate, query, tail_ss)
    ss = lax.all_gather(ss[0], "tp")
    return normalize(ss, head, tail, gain, channels * lax.axis_size("tp"))


def solution(mesh):
    in_specs = (
        P("ctx", "tp"),
        P("ctx", None, "tp"),
        P(None, None, "tp"),
        P("tp", None),
        P("tp"),
        P("tp"),
    )
    return jax.shard_map(
        on_device, mesh=mesh, in_specs=in_specs, out_specs=P("ctx", "tp"), check_vma=False
    )
```

```python
import functools

import jax
import jax.numpy as jnp
from jax import lax
from jax.experimental import pallas as pl
from jax.experimental.pallas import tpu as pltpu
from jax.sharding import PartitionSpec as P

F32 = jnp.float32
BF16 = jnp.bfloat16
LANES = 128
HEAD = 80
TAIL = 48
EPS = 1e-06
WIDTHS = (768, 768, 512)
UNROLL = 2
NORM_BLOCKS = 4
VMEM = pl.BlockSpec(memory_space=pltpu.VMEM)
MIB = 1 << 20


def in_hbm(x):
    return pltpu.with_memory_space_constraint(x, pltpu.HBM)


def causal3(x, w):
    return w[0] * x + w[1] * pltpu.roll(x, 1, 0) + w[2] * pltpu.roll(x, 2, 0)


def gate_tile(load_kv, last_q, taps, halo):
    raw = [load_kv(s).astype(F32) for s in range(2)]
    feat = [causal3(raw[s], taps[s])[halo:] for s in range(2)]
    gate = (feat[0] * feat[1]).astype(BF16)
    last_q = pltpu.roll(last_q.astype(F32)[-8:], 2, 0)
    last_k = pltpu.roll(raw[0][-8:], 4, 0)
    last_v = pltpu.roll(raw[1][-8:], 6, 0)
    row = lax.broadcasted_iota(jnp.int32, last_q.shape, 0)
    rim = jnp.where(row < 2, last_q, jnp.where(row < 4, last_k, jnp.where(row < 6, last_v, 0.0)))
    return gate, rim.astype(BF16)


def tail_gate_kernel(begin, feats_ref, short_ref, out_ref, kv_ref, q_ref, taps_ref, sem):
    rows = feats_ref.shape[1]
    width = out_ref.shape[1]
    halo = kv_ref.shape[1] - LANES
    here = pl.ds(begin, width)
    copies = [
        pltpu.make_async_copy(feats_ref.at[pl.ds(1, 2), pl.ds(rows - LANES - halo, LANES + halo), here], kv_ref, sem.at[0]),
        pltpu.make_async_copy(feats_ref.at[0, pl.ds(rows - 16, 16), here], q_ref, sem.at[1]),
        pltpu.make_async_copy(short_ref.at[:, :, here], taps_ref, sem.at[2]),
    ]
    for copy in copies:
        copy.start()
    for copy in copies:
        copy.wait()
    for t in range(width // LANES):
        lanes = slice(t * LANES, (t + 1) * LANES)
        taps = [[taps_ref[i, s : s + 1, lanes] for i in range(3)] for s in (1, 2)]
        gate, rim = gate_tile(lambda s: kv_ref[s, :, lanes], q_ref[:, lanes], taps, halo)
        out_ref[:LANES, lanes] = gate
        out_ref[LANES:, lanes] = rim


def tail_gate(feats, short_taps, begin, width):
    halo = 16
    return pl.pallas_call(
        functools.partial(tail_gate_kernel, begin),
        in_specs=[pl.BlockSpec(memory_space=pltpu.HBM)] * 2,
        out_specs=VMEM,
        out_shape=jax.ShapeDtypeStruct((LANES + 8, width), BF16),
        scratch_shapes=[
            pltpu.VMEM((2, LANES + halo, width), BF16),
            pltpu.VMEM((16, width), BF16),
            pltpu.VMEM((3, 3, width), F32),
            pltpu.SemaphoreType.DMA((3,)),
        ],
        compiler_params=pltpu.CompilerParams(vmem_limit_bytes=4 * MIB),
        name="tail_gate",
    )(in_hbm(feats), in_hbm(short_taps))


def group_select(prod, per_tile, rows):
    lane = lax.broadcasted_iota(jnp.int32, (rows, 2 * LANES), 1)
    owner = (lane % LANES) // (LANES // per_tile)
    acc = prod[:rows]
    for g in range(1, per_tile):
        acc = jnp.where(owner == g, prod[g * rows : (g + 1) * rows], acc)
    return jnp.concatenate([acc[:, :LANES], acc[:, LANES:]], 0)


def local_kernel(
    hbm_ref, res_ref, short_ref, filt_ref, skip_ref, toep_ref, gate_ref, q_ref, first_ref, stream_ref, ss_ref, feats_ref, sem
):
    tokens, channels = res_ref.shape
    part = UNROLL * LANES

    def load(p):
        lanes = pl.ds(pl.multiple_of(p * part, part), part)
        return pltpu.make_async_copy(hbm_ref.at[:, :, lanes], feats_ref.at[:, :, lanes], sem.at[p])

    for p in range(channels // part):
        load(p).start()
    tiles = channels // LANES
    per_tile = filt_ref.shape[0] // tiles
    first = tokens - 2 * TAIL
    tap = lax.broadcasted_iota(jnp.int32, (LANES, 2 * LANES), 0)
    pos = lax.broadcasted_iota(jnp.int32, (LANES, 2 * LANES), 1)
    flip = (tap + pos == LANES).astype(BF16)

    def tile(t):
        lanes = pl.ds(pl.multiple_of(t * LANES, LANES), LANES)
        first_ref[:, :, lanes] = feats_ref[:, : first_ref.shape[1], lanes]
        feats = [
            causal3(feats_ref[s, :, lanes].astype(F32), [short_ref[i, s : s + 1, lanes] for i in range(3)])
            for s in range(3)
        ]
        gate = (feats[1] * feats[2]).astype(BF16)
        gate_ref[:, lanes] = gate
        q_ref[:, lanes] = feats[0].astype(BF16)
        taps = filt_ref[pl.ds(pl.multiple_of(t * per_tile, per_tile), per_tile), :]
        base = jnp.dot(taps, flip, preferred_element_type=F32)
        lhs = []
        for g in range(per_tile):
            wide = jnp.broadcast_to(base[g : g + 1], (HEAD, 2 * LANES))
            band = pltpu.roll(wide, 0, 1, stride=1, stride_axis=0).astype(BF16)
            toep_ref[t, g * HEAD : (g + 1) * HEAD, :] = band
            lhs.append(band[:TAIL])
        z0 = jnp.zeros((first - LANES, LANES), BF16)
        z1 = jnp.zeros((first - LANES + TAIL, LANES), BF16)
        rhs = jnp.concatenate(
            [
                jnp.concatenate([gate[first - LANES :], z0], 0),
                jnp.concatenate([gate[first - LANES + TAIL :], z1], 0),
            ],
            1,
        )
        prod = jnp.dot(jnp.concatenate(lhs, 0), rhs, preferred_element_type=F32)
        filtered = group_select(prod, per_tile, TAIL)
        filtered = filtered + skip_ref[:, lanes] * gate[first:].astype(F32)
        stream = (res_ref[first:, lanes].astype(F32) + feats[0][first:] * filtered).astype(BF16)
        stream_ref[:, lanes] = stream
        wide_stream = stream.astype(F32)
        return wide_stream * wide_stream

    def step(p, total):
        load(p).wait()
        for u in range(UNROLL):
            total = total + tile(p * UNROLL + u)
        return total

    ss_ref[...] = lax.fori_loop(0, tiles // UNROLL, step, jnp.zeros((2 * TAIL, LANES), F32))


def local_part(feats, residual, short_taps, filter_taps, skip):
    _, tokens, channels = feats.shape
    tiles = channels // LANES
    per_tile = filter_taps.shape[0] // tiles
    return pl.pallas_call(
        local_kernel,
        in_specs=[pl.BlockSpec(memory_space=pltpu.HBM)] + [VMEM] * 4,
        out_specs=[VMEM] * 6,
        out_shape=[
            jax.ShapeDtypeStruct((tiles, per_tile * HEAD, 2 * LANES), BF16),
            jax.ShapeDtypeStruct((tokens, channels), BF16),
            jax.ShapeDtypeStruct((tokens, channels), BF16),
            jax.ShapeDtypeStruct((3, 16, channels), BF16),
            jax.ShapeDtypeStruct((2 * TAIL, channels), BF16),
            jax.ShapeDtypeStruct((2 * TAIL, LANES), F32),
        ],
        scratch_shapes=[
            pltpu.VMEM(feats.shape, BF16),
            pltpu.SemaphoreType.DMA((channels // (UNROLL * LANES),)),
        ],
        compiler_params=pltpu.CompilerParams(vmem_limit_bytes=16 * MIB),
        cost_estimate=pl.CostEstimate(flops=10**9, transcendentals=0, bytes_accessed=16 * MIB),
        name="local_part",
    )(in_hbm(feats), residual, short_taps, filter_taps, skip)


def head_kernel(start, carry_ref, first_ref, res_ref, short_ref, skip_ref, toep_ref, gate_ref, q_ref, before_ref, stream_ref, ss_ref):
    per_tile = toep_ref.shape[1] // HEAD
    rows = 2 * HEAD
    row = lax.broadcasted_iota(jnp.int32, (16, LANES), 0)
    total = before_ref[-rows:] if before_ref.shape[0] >= rows else jnp.zeros((rows, LANES), F32)
    for c in range(carry_ref.shape[1] // LANES):
        near = slice(c * LANES, (c + 1) * LANES)
        lanes = slice(start + c * LANES, start + (c + 1) * LANES)
        rim = carry_ref[LANES:, near].astype(F32)
        carry = carry_ref[:LANES, near]
        feats = []
        for s in range(3):
            x = first_ref[s, :, lanes].astype(F32)
            w = [short_ref[i, s : s + 1, lanes] for i in range(3)]
            older, newer = rim[2 * s : 2 * s + 1], rim[2 * s + 1 : 2 * s + 2]
            x1 = jnp.where(row == 0, newer, pltpu.roll(x, 1, 0))
            x2 = jnp.where(row == 0, older, jnp.where(row == 1, newer, pltpu.roll(x, 2, 0)))
            feats.append(w[0] * x + w[1] * x1 + w[2] * x2)
        fixed = (feats[1] * feats[2]).astype(BF16)
        gate = jnp.concatenate([fixed, gate_ref[16 : LANES + HEAD, lanes]], 0)
        query = jnp.concatenate([feats[0].astype(BF16), q_ref[16:rows, lanes]], 0)
        rhs = jnp.concatenate(
            [jnp.concatenate([carry, gate[:LANES]], 0), jnp.concatenate([carry[HEAD:], gate], 0)], 1
        )
        prod = jnp.dot(toep_ref[start // LANES + c], rhs, preferred_element_type=F32)
        filtered = group_select(prod, per_tile, HEAD)
        filtered = filtered + skip_ref[:, lanes] * gate[:rows].astype(F32)
        stream = (res_ref[:rows, lanes].astype(F32) + query.astype(F32) * filtered).astype(BF16)
        stream_ref[:, near] = stream
        wide_stream = stream.astype(F32)
        total = total + wide_stream * wide_stream
    if ss_ref.shape[0] == 8:
        total = jnp.concatenate([total, before_ref[: 2 * TAIL]], 0)
        sums = jnp.sum(jnp.transpose(total), axis=0, keepdims=True)
        ss_ref[...] = jnp.broadcast_to(sums, ss_ref.shape)
    else:
        ss_ref[: 2 * TAIL] = before_ref[: 2 * TAIL]
        ss_ref[2 * TAIL :] = total


def head_part(start, last, carry, first, residual, short_taps, skip, toep, gate, query, before):
    tokens = residual.shape[0]
    ss_shape = (8, tokens) if last else (tokens, LANES)
    return pl.pallas_call(
        functools.partial(head_kernel, start),
        in_specs=[VMEM] * 9,
        out_specs=[VMEM] * 2,
        out_shape=[
            jax.ShapeDtypeStruct((2 * HEAD, carry.shape[1]), BF16),
            jax.ShapeDtypeStruct(ss_shape, F32),
        ],
        compiler_params=pltpu.CompilerParams(vmem_limit_bytes=8 * MIB),
        name="head_part",
    )(carry, first, residual, short_taps, skip, toep, gate, query, before)


def norm_kernel(width, ss_ref, *refs):
    *head_refs, tail_ref, gain_ref, out_ref, buf, sem = refs
    tokens = buf.shape[0]
    split = head_refs[0].shape[0]
    sums = jnp.sum(ss_ref[...], axis=0, keepdims=True)
    scale = jnp.transpose(jnp.broadcast_to(lax.rsqrt(sums / width + EPS), (LANES, tokens)))
    copies = []
    step = tokens // NORM_BLOCKS
    for b in range(NORM_BLOCKS):
        begin, end = b * step, (b + 1) * step
        for low, high, offset, refs_here in (
            (begin, min(end, split), 0, head_refs),
            (max(begin, split), end, split, [tail_ref]),
        ):
            if high <= low:
                continue
            base = 0
            for ref in refs_here:
                for t in range(ref.shape[1] // LANES):
                    near = slice(t * LANES, (t + 1) * LANES)
                    lanes = slice(base + t * LANES, base + (t + 1) * LANES)
                    value = ref[low - offset : high - offset, near].astype(F32)
                    buf[low:high, lanes] = (value * scale[low:high] * gain_ref[:, lanes]).astype(BF16)
                base += ref.shape[1]
        copy = pltpu.make_async_copy(buf.at[begin:end], out_ref.at[begin:end], sem.at[b])
        copy.start()
        copies.append(copy)
    for copy in copies:
        copy.wait()


def normalize(ss, heads, tail, gain, width):
    tokens = heads[0].shape[0] + tail.shape[0]
    channels = tail.shape[1]
    return pl.pallas_call(
        functools.partial(norm_kernel, width),
        in_specs=[VMEM] * (3 + len(heads)),
        out_specs=pl.BlockSpec(memory_space=pl.ANY),
        out_shape=jax.ShapeDtypeStruct((tokens, channels), BF16),
        scratch_shapes=[pltpu.VMEM((tokens, channels), BF16), pltpu.SemaphoreType.DMA((NORM_BLOCKS,))],
        compiler_params=pltpu.CompilerParams(vmem_limit_bytes=8 * MIB),
        name="normalize",
    )(ss, *heads, tail, gain)


def on_device(residual, features, short_taps, filter_taps, skip_gain, norm_gain):
    channels = residual.shape[1]
    feats = jnp.transpose(features, (1, 0, 2))
    skip = skip_gain.reshape(1, channels)
    gain = norm_gain.reshape(1, channels)
    size = lax.axis_size("ctx")
    route = [(i, i + 1) for i in range(size - 1)]
    starts = [sum(WIDTHS[:i]) for i in range(len(WIDTHS))]
    parts = [tail_gate(feats, short_taps, s, w) for s, w in zip(starts, WIDTHS)]
    carries = [lax.ppermute(part, "ctx", route) for part in parts]
    toep, gate, query, first, tail, ss = local_part(feats, residual, short_taps, filter_taps, skip)
    heads = []
    for start, carry in zip(starts, carries):
        last = start + carry.shape[1] == channels
        head, ss = head_part(start, last, carry, first, residual, short_taps, skip, toep, gate, query, ss)
        heads.append(head)
    ss = lax.all_gather(ss[0], "tp")
    return normalize(ss, heads, tail, gain, channels * lax.axis_size("tp"))


def solution(mesh):
    in_specs = (
        P("ctx", "tp"),
        P("ctx", None, "tp"),
        P(None, None, "tp"),
        P("tp", None),
        P("tp"),
        P("tp"),
    )
    return jax.shard_map(
        on_device, mesh=mesh, in_specs=in_specs, out_specs=P("ctx", "tp"), check_vma=False
    )
```

```python
import functools

import jax
import jax.numpy as jnp
from jax import lax
from jax.experimental import pallas as pl
from jax.experimental.pallas import tpu as pltpu
from jax.sharding import PartitionSpec as P

F32 = jnp.float32
BF16 = jnp.bfloat16
LANES = 128
HEAD = 80
TAIL = 48
EPS = 1e-06
WIDTHS = (896, 896, 256)
UNROLL = 2
NORM_BLOCKS = 4
VMEM = pl.BlockSpec(memory_space=pltpu.VMEM)
MIB = 1 << 20


def in_hbm(x):
    return pltpu.with_memory_space_constraint(x, pltpu.HBM)


def causal3(x, w):
    return w[0] * x + w[1] * pltpu.roll(x, 1, 0) + w[2] * pltpu.roll(x, 2, 0)


def gate_tile(load_kv, last_q, taps, halo):
    raw = [load_kv(s).astype(F32) for s in range(2)]
    feat = [causal3(raw[s], taps[s])[halo:] for s in range(2)]
    gate = (feat[0] * feat[1]).astype(BF16)
    last_q = pltpu.roll(last_q.astype(F32)[-8:], 2, 0)
    last_k = pltpu.roll(raw[0][-8:], 4, 0)
    last_v = pltpu.roll(raw[1][-8:], 6, 0)
    row = lax.broadcasted_iota(jnp.int32, last_q.shape, 0)
    rim = jnp.where(row < 2, last_q, jnp.where(row < 4, last_k, jnp.where(row < 6, last_v, 0.0)))
    return gate, rim.astype(BF16)


def tail_gate_kernel(begin, feats_ref, short_ref, out_ref, kv_ref, q_ref, taps_ref, sem):
    rows = feats_ref.shape[1]
    width = out_ref.shape[1]
    halo = kv_ref.shape[1] - LANES
    here = pl.ds(begin, width)
    copies = [
        pltpu.make_async_copy(feats_ref.at[pl.ds(1, 2), pl.ds(rows - LANES - halo, LANES + halo), here], kv_ref, sem.at[0]),
        pltpu.make_async_copy(feats_ref.at[0, pl.ds(rows - 16, 16), here], q_ref, sem.at[1]),
        pltpu.make_async_copy(short_ref.at[:, :, here], taps_ref, sem.at[2]),
    ]
    for copy in copies:
        copy.start()
    for copy in copies:
        copy.wait()
    for t in range(width // LANES):
        lanes = slice(t * LANES, (t + 1) * LANES)
        taps = [[taps_ref[i, s : s + 1, lanes] for i in range(3)] for s in (1, 2)]
        gate, rim = gate_tile(lambda s: kv_ref[s, :, lanes], q_ref[:, lanes], taps, halo)
        out_ref[:LANES, lanes] = gate
        out_ref[LANES:, lanes] = rim


def tail_gate(feats, short_taps, begin, width):
    halo = 8
    return pl.pallas_call(
        functools.partial(tail_gate_kernel, begin),
        in_specs=[pl.BlockSpec(memory_space=pltpu.HBM)] * 2,
        out_specs=VMEM,
        out_shape=jax.ShapeDtypeStruct((LANES + 8, width), BF16),
        scratch_shapes=[
            pltpu.VMEM((2, LANES + halo, width), BF16),
            pltpu.VMEM((16, width), BF16),
            pltpu.VMEM((3, 3, width), F32),
            pltpu.SemaphoreType.DMA((3,)),
        ],
        compiler_params=pltpu.CompilerParams(vmem_limit_bytes=4 * MIB),
        name="tail_gate",
    )(in_hbm(feats), in_hbm(short_taps))


def group_select(prod, per_tile, rows):
    lane = lax.broadcasted_iota(jnp.int32, (rows, 2 * LANES), 1)
    owner = (lane % LANES) // (LANES // per_tile)
    acc = prod[:rows]
    for g in range(1, per_tile):
        acc = jnp.where(owner == g, prod[g * rows : (g + 1) * rows], acc)
    return jnp.concatenate([acc[:, :LANES], acc[:, LANES:]], 0)


def local_kernel(
    hbm_ref, res_ref, short_ref, filt_ref, skip_ref, toep_ref, gate_ref, q_ref, first_ref, stream_ref, ss_ref, feats_ref, sem
):
    tokens, channels = res_ref.shape
    part = UNROLL * LANES

    def load(p):
        lanes = pl.ds(pl.multiple_of(p * part, part), part)
        return pltpu.make_async_copy(hbm_ref.at[:, :, lanes], feats_ref.at[:, :, lanes], sem.at[p])

    for p in range(channels // part):
        load(p).start()
    tiles = channels // LANES
    per_tile = filt_ref.shape[0] // tiles
    first = tokens - 2 * TAIL
    tap = lax.broadcasted_iota(jnp.int32, (LANES, 2 * LANES), 0)
    pos = lax.broadcasted_iota(jnp.int32, (LANES, 2 * LANES), 1)
    flip = (tap + pos == LANES).astype(BF16)

    def tile(t):
        lanes = pl.ds(pl.multiple_of(t * LANES, LANES), LANES)
        first_ref[:, :, lanes] = feats_ref[:, : first_ref.shape[1], lanes]
        feats = [
            causal3(feats_ref[s, :, lanes].astype(F32), [short_ref[i, s : s + 1, lanes] for i in range(3)])
            for s in range(3)
        ]
        gate = (feats[1] * feats[2]).astype(BF16)
        gate_ref[:, lanes] = gate
        q_ref[:, lanes] = feats[0].astype(BF16)
        taps = filt_ref[pl.ds(pl.multiple_of(t * per_tile, per_tile), per_tile), :]
        base = jnp.dot(taps, flip, preferred_element_type=F32)
        lhs = []
        for g in range(per_tile):
            wide = jnp.broadcast_to(base[g : g + 1], (HEAD, 2 * LANES))
            band = pltpu.roll(wide, 0, 1, stride=1, stride_axis=0).astype(BF16)
            toep_ref[t, g * HEAD : (g + 1) * HEAD, :] = band
            lhs.append(band[:TAIL])
        z0 = jnp.zeros((first - LANES, LANES), BF16)
        z1 = jnp.zeros((first - LANES + TAIL, LANES), BF16)
        rhs = jnp.concatenate(
            [
                jnp.concatenate([gate[first - LANES :], z0], 0),
                jnp.concatenate([gate[first - LANES + TAIL :], z1], 0),
            ],
            1,
        )
        prod = jnp.dot(jnp.concatenate(lhs, 0), rhs, preferred_element_type=F32)
        filtered = group_select(prod, per_tile, TAIL)
        filtered = filtered + skip_ref[:, lanes] * gate[first:].astype(F32)
        stream = (res_ref[first:, lanes].astype(F32) + feats[0][first:] * filtered).astype(BF16)
        stream_ref[:, lanes] = stream
        wide_stream = stream.astype(F32)
        return wide_stream * wide_stream

    def step(p, total):
        load(p).wait()
        for u in range(UNROLL):
            total = total + tile(p * UNROLL + u)
        return total

    ss_ref[...] = lax.fori_loop(0, tiles // UNROLL, step, jnp.zeros((2 * TAIL, LANES), F32))


def local_part(feats, residual, short_taps, filter_taps, skip):
    _, tokens, channels = feats.shape
    tiles = channels // LANES
    per_tile = filter_taps.shape[0] // tiles
    return pl.pallas_call(
        local_kernel,
        in_specs=[pl.BlockSpec(memory_space=pltpu.HBM)] + [VMEM] * 4,
        out_specs=[VMEM] * 6,
        out_shape=[
            jax.ShapeDtypeStruct((tiles, per_tile * HEAD, 2 * LANES), BF16),
            jax.ShapeDtypeStruct((tokens, channels), BF16),
            jax.ShapeDtypeStruct((tokens, channels), BF16),
            jax.ShapeDtypeStruct((3, 16, channels), BF16),
            jax.ShapeDtypeStruct((2 * TAIL, channels), BF16),
            jax.ShapeDtypeStruct((2 * TAIL, LANES), F32),
        ],
        scratch_shapes=[
            pltpu.VMEM(feats.shape, BF16),
            pltpu.SemaphoreType.DMA((channels // (UNROLL * LANES),)),
        ],
        compiler_params=pltpu.CompilerParams(vmem_limit_bytes=16 * MIB),
        cost_estimate=pl.CostEstimate(flops=10**9, transcendentals=0, bytes_accessed=16 * MIB),
        name="local_part",
    )(in_hbm(feats), residual, short_taps, filter_taps, skip)


def head_kernel(start, carry_ref, first_ref, res_ref, short_ref, skip_ref, toep_ref, gate_ref, q_ref, before_ref, stream_ref, ss_ref):
    per_tile = toep_ref.shape[1] // HEAD
    rows = 2 * HEAD
    row = lax.broadcasted_iota(jnp.int32, (16, LANES), 0)
    total = before_ref[-rows:] if before_ref.shape[0] >= rows else jnp.zeros((rows, LANES), F32)
    for c in range(carry_ref.shape[1] // LANES):
        near = slice(c * LANES, (c + 1) * LANES)
        lanes = slice(start + c * LANES, start + (c + 1) * LANES)
        rim = carry_ref[LANES:, near].astype(F32)
        carry = carry_ref[:LANES, near]
        feats = []
        for s in range(3):
            x = first_ref[s, :, lanes].astype(F32)
            w = [short_ref[i, s : s + 1, lanes] for i in range(3)]
            older, newer = rim[2 * s : 2 * s + 1], rim[2 * s + 1 : 2 * s + 2]
            x1 = jnp.where(row == 0, newer, pltpu.roll(x, 1, 0))
            x2 = jnp.where(row == 0, older, jnp.where(row == 1, newer, pltpu.roll(x, 2, 0)))
            feats.append(w[0] * x + w[1] * x1 + w[2] * x2)
        fixed = (feats[1] * feats[2]).astype(BF16)
        gate = jnp.concatenate([fixed, gate_ref[16 : LANES + HEAD, lanes]], 0)
        query = jnp.concatenate([feats[0].astype(BF16), q_ref[16:rows, lanes]], 0)
        rhs = jnp.concatenate(
            [jnp.concatenate([carry, gate[:LANES]], 0), jnp.concatenate([carry[HEAD:], gate], 0)], 1
        )
        prod = jnp.dot(toep_ref[start // LANES + c], rhs, preferred_element_type=F32)
        filtered = group_select(prod, per_tile, HEAD)
        filtered = filtered + skip_ref[:, lanes] * gate[:rows].astype(F32)
        stream = (res_ref[:rows, lanes].astype(F32) + query.astype(F32) * filtered).astype(BF16)
        stream_ref[:, near] = stream
        wide_stream = stream.astype(F32)
        total = total + wide_stream * wide_stream
    if ss_ref.shape[0] == 8:
        total = jnp.concatenate([total, before_ref[: 2 * TAIL]], 0)
        sums = jnp.sum(jnp.transpose(total), axis=0, keepdims=True)
        ss_ref[...] = jnp.broadcast_to(sums, ss_ref.shape)
    else:
        ss_ref[: 2 * TAIL] = before_ref[: 2 * TAIL]
        ss_ref[2 * TAIL :] = total


def head_part(start, last, carry, first, residual, short_taps, skip, toep, gate, query, before):
    tokens = residual.shape[0]
    ss_shape = (8, tokens) if last else (tokens, LANES)
    return pl.pallas_call(
        functools.partial(head_kernel, start),
        in_specs=[VMEM] * 9,
        out_specs=[VMEM] * 2,
        out_shape=[
            jax.ShapeDtypeStruct((2 * HEAD, carry.shape[1]), BF16),
            jax.ShapeDtypeStruct(ss_shape, F32),
        ],
        compiler_params=pltpu.CompilerParams(vmem_limit_bytes=8 * MIB),
        name="head_part",
    )(carry, first, residual, short_taps, skip, toep, gate, query, before)


def norm_kernel(width, ss_ref, *refs):
    *head_refs, tail_ref, gain_ref, out_ref, buf, sem = refs
    tokens = buf.shape[0]
    split = head_refs[0].shape[0]
    sums = jnp.sum(ss_ref[...], axis=0, keepdims=True)
    scale = jnp.transpose(jnp.broadcast_to(lax.rsqrt(sums / width + EPS), (LANES, tokens)))
    copies = []
    step = tokens // NORM_BLOCKS
    for b in range(NORM_BLOCKS):
        begin, end = b * step, (b + 1) * step
        for low, high, offset, refs_here in (
            (begin, min(end, split), 0, head_refs),
            (max(begin, split), end, split, [tail_ref]),
        ):
            if high <= low:
                continue
            base = 0
            for ref in refs_here:
                for t in range(ref.shape[1] // LANES):
                    near = slice(t * LANES, (t + 1) * LANES)
                    lanes = slice(base + t * LANES, base + (t + 1) * LANES)
                    value = ref[low - offset : high - offset, near].astype(F32)
                    buf[low:high, lanes] = (value * scale[low:high] * gain_ref[:, lanes]).astype(BF16)
                base += ref.shape[1]
        copy = pltpu.make_async_copy(buf.at[begin:end], out_ref.at[begin:end], sem.at[b])
        copy.start()
        copies.append(copy)
    for copy in copies:
        copy.wait()


def normalize(ss, heads, tail, gain, width):
    tokens = heads[0].shape[0] + tail.shape[0]
    channels = tail.shape[1]
    return pl.pallas_call(
        functools.partial(norm_kernel, width),
        in_specs=[VMEM] * (3 + len(heads)),
        out_specs=pl.BlockSpec(memory_space=pl.ANY),
        out_shape=jax.ShapeDtypeStruct((tokens, channels), BF16),
        scratch_shapes=[pltpu.VMEM((tokens, channels), BF16), pltpu.SemaphoreType.DMA((NORM_BLOCKS,))],
        compiler_params=pltpu.CompilerParams(vmem_limit_bytes=8 * MIB),
        name="normalize",
    )(ss, *heads, tail, gain)


def on_device(residual, features, short_taps, filter_taps, skip_gain, norm_gain):
    channels = residual.shape[1]
    feats = jnp.transpose(features, (1, 0, 2))
    skip = skip_gain.reshape(1, channels)
    gain = norm_gain.reshape(1, channels)
    size = lax.axis_size("ctx")
    route = [(i, i + 1) for i in range(size - 1)]
    starts = [sum(WIDTHS[:i]) for i in range(len(WIDTHS))]
    parts = [tail_gate(feats, short_taps, s, w) for s, w in zip(starts, WIDTHS)]
    cut = size // 2 - 1
    early = [pair for pair in route if pair != (cut - 1, cut)]
    carries = [lax.ppermute(part, "ctx", route if i else early) for i, part in enumerate(parts)]
    carries[0] = carries[0] + lax.ppermute(parts[0], "ctx", [(cut - 1, cut)])
    toep, gate, query, first, tail, ss = local_part(feats, residual, short_taps, filter_taps, skip)
    heads = []
    for start, carry in zip(starts, carries):
        last = start + carry.shape[1] == channels
        head, ss = head_part(start, last, carry, first, residual, short_taps, skip, toep, gate, query, ss)
        heads.append(head)
    ss = lax.all_gather(ss[0], "tp")
    return normalize(ss, heads, tail, gain, channels * lax.axis_size("tp"))


def solution(mesh):
    in_specs = (
        P("ctx", "tp"),
        P("ctx", None, "tp"),
        P(None, None, "tp"),
        P("tp", None),
        P("tp"),
        P("tp"),
    )
    return jax.shard_map(
        on_device, mesh=mesh, in_specs=in_specs, out_specs=P("ctx", "tp"), check_vma=False
    )
```

```python
import functools

import jax
import jax.numpy as jnp
from jax import lax
from jax.experimental import pallas as pl
from jax.experimental.pallas import tpu as pltpu
from jax.sharding import PartitionSpec as P

F32 = jnp.float32
BF16 = jnp.bfloat16
LANES = 128
HEAD = 80
TAIL = 48
EPS = 1e-06
WIDTHS = (896, 896, 256)
UNROLL = 2
NORM_BLOCKS = 8
VMEM = pl.BlockSpec(memory_space=pltpu.VMEM)
MIB = 1 << 20


def in_hbm(x):
    return pltpu.with_memory_space_constraint(x, pltpu.HBM)


def rounded(x):
    return x.astype(BF16).astype(F32)


def causal3(x, w):
    return w[0] * x + w[1] * pltpu.roll(x, 1, 0) + w[2] * pltpu.roll(x, 2, 0)


def gate_tile(load_kv, last_q, taps, halo):
    raw = [load_kv(s).astype(F32) for s in range(2)]
    feat = [causal3(raw[s], taps[s])[halo:] for s in range(2)]
    gate = (rounded(feat[0]) * rounded(feat[1])).astype(BF16)
    last_q = pltpu.roll(last_q.astype(F32)[-8:], 2, 0)
    last_k = pltpu.roll(raw[0][-8:], 4, 0)
    last_v = pltpu.roll(raw[1][-8:], 6, 0)
    row = lax.broadcasted_iota(jnp.int32, last_q.shape, 0)
    rim = jnp.where(row < 2, last_q, jnp.where(row < 4, last_k, jnp.where(row < 6, last_v, 0.0)))
    return gate, rim.astype(BF16)


def tail_gate_kernel(begin, feats_ref, short_ref, out_ref, kv_ref, q_ref, taps_ref, sem):
    rows = feats_ref.shape[1]
    width = out_ref.shape[1]
    halo = kv_ref.shape[1] - LANES
    here = pl.ds(begin, width)
    copies = [
        pltpu.make_async_copy(feats_ref.at[pl.ds(1, 2), pl.ds(rows - LANES - halo, LANES + halo), here], kv_ref, sem.at[0]),
        pltpu.make_async_copy(feats_ref.at[0, pl.ds(rows - 16, 16), here], q_ref, sem.at[1]),
        pltpu.make_async_copy(short_ref.at[:, :, here], taps_ref, sem.at[2]),
    ]
    for copy in copies:
        copy.start()
    for copy in copies:
        copy.wait()
    for t in range(width // LANES):
        lanes = slice(t * LANES, (t + 1) * LANES)
        taps = [[taps_ref[i, s : s + 1, lanes] for i in range(3)] for s in (1, 2)]
        gate, rim = gate_tile(lambda s: kv_ref[s, :, lanes], q_ref[:, lanes], taps, halo)
        out_ref[:LANES, lanes] = gate
        out_ref[LANES:, lanes] = rim


def tail_gate(feats, short_taps, begin, width):
    halo = 8
    return pl.pallas_call(
        functools.partial(tail_gate_kernel, begin),
        in_specs=[pl.BlockSpec(memory_space=pltpu.HBM)] * 2,
        out_specs=VMEM,
        out_shape=jax.ShapeDtypeStruct((LANES + 8, width), BF16),
        scratch_shapes=[
            pltpu.VMEM((2, LANES + halo, width), BF16),
            pltpu.VMEM((16, width), BF16),
            pltpu.VMEM((3, 3, width), F32),
            pltpu.SemaphoreType.DMA((3,)),
        ],
        compiler_params=pltpu.CompilerParams(vmem_limit_bytes=4 * MIB),
        name="tail_gate",
    )(in_hbm(feats), in_hbm(short_taps))


def group_select(prod, per_tile, rows):
    lane = lax.broadcasted_iota(jnp.int32, (rows, 2 * LANES), 1)
    owner = (lane % LANES) // (LANES // per_tile)
    acc = prod[:rows]
    for g in range(1, per_tile):
        acc = jnp.where(owner == g, prod[g * rows : (g + 1) * rows], acc)
    return jnp.concatenate([acc[:, :LANES], acc[:, LANES:]], 0)


def local_kernel(
    hbm_ref, res_ref, short_ref, filt_ref, skip_ref, toep_ref, gate_ref, q_ref, first_ref, stream_ref, ss_ref, feats_ref, sem
):
    tokens, channels = res_ref.shape
    part = UNROLL * LANES

    def load(p):
        lanes = pl.ds(pl.multiple_of(p * part, part), part)
        return pltpu.make_async_copy(hbm_ref.at[:, :, lanes], feats_ref.at[:, :, lanes], sem.at[p])

    for p in range(channels // part):
        load(p).start()
    tiles = channels // LANES
    per_tile = filt_ref.shape[0] // tiles
    first = tokens - 2 * TAIL
    tap = lax.broadcasted_iota(jnp.int32, (LANES, 2 * LANES), 0)
    pos = lax.broadcasted_iota(jnp.int32, (LANES, 2 * LANES), 1)
    flip = (tap + pos == LANES).astype(BF16)

    def tile(t):
        lanes = pl.ds(pl.multiple_of(t * LANES, LANES), LANES)
        first_ref[:, :, lanes] = feats_ref[:, : first_ref.shape[1], lanes]
        feats = [
            causal3(feats_ref[s, :, lanes].astype(F32), [short_ref[i, s : s + 1, lanes] for i in range(3)])
            for s in range(3)
        ]
        gate = (rounded(feats[1]) * rounded(feats[2])).astype(BF16)
        query = feats[0].astype(BF16)
        gate_ref[:, lanes] = gate
        q_ref[:, lanes] = query
        taps = filt_ref[pl.ds(pl.multiple_of(t * per_tile, per_tile), per_tile), :]
        base = jnp.dot(taps, flip, preferred_element_type=F32)
        lhs = []
        for g in range(per_tile):
            wide = jnp.broadcast_to(base[g : g + 1], (HEAD, 2 * LANES))
            band = pltpu.roll(wide, 0, 1, stride=1, stride_axis=0).astype(BF16)
            toep_ref[t, g * HEAD : (g + 1) * HEAD, :] = band
            lhs.append(band[:TAIL])
        z0 = jnp.zeros((first - LANES, LANES), BF16)
        z1 = jnp.zeros((first - LANES + TAIL, LANES), BF16)
        rhs = jnp.concatenate(
            [
                jnp.concatenate([gate[first - LANES :], z0], 0),
                jnp.concatenate([gate[first - LANES + TAIL :], z1], 0),
            ],
            1,
        )
        prod = jnp.dot(jnp.concatenate(lhs, 0), rhs, preferred_element_type=F32)
        filtered = group_select(prod, per_tile, TAIL)
        filtered = filtered + skip_ref[:, lanes] * gate[first:].astype(F32)
        stream = (res_ref[first:, lanes].astype(F32) + query[first:].astype(F32) * filtered).astype(BF16)
        stream_ref[:, lanes] = stream
        wide_stream = stream.astype(F32)
        return wide_stream * wide_stream

    def step(p, total):
        load(p).wait()
        for u in range(UNROLL):
            total = total + tile(p * UNROLL + u)
        return total

    ss_ref[...] = lax.fori_loop(0, tiles // UNROLL, step, jnp.zeros((2 * TAIL, LANES), F32))


def local_part(feats, residual, short_taps, filter_taps, skip):
    _, tokens, channels = feats.shape
    tiles = channels // LANES
    per_tile = filter_taps.shape[0] // tiles
    return pl.pallas_call(
        local_kernel,
        in_specs=[pl.BlockSpec(memory_space=pltpu.HBM)] + [VMEM] * 4,
        out_specs=[VMEM] * 6,
        out_shape=[
            jax.ShapeDtypeStruct((tiles, per_tile * HEAD, 2 * LANES), BF16),
            jax.ShapeDtypeStruct((tokens, channels), BF16),
            jax.ShapeDtypeStruct((tokens, channels), BF16),
            jax.ShapeDtypeStruct((3, 16, channels), BF16),
            jax.ShapeDtypeStruct((2 * TAIL, channels), BF16),
            jax.ShapeDtypeStruct((2 * TAIL, LANES), F32),
        ],
        scratch_shapes=[
            pltpu.VMEM(feats.shape, BF16),
            pltpu.SemaphoreType.DMA((channels // (UNROLL * LANES),)),
        ],
        compiler_params=pltpu.CompilerParams(vmem_limit_bytes=16 * MIB),
        cost_estimate=pl.CostEstimate(flops=10**9, transcendentals=0, bytes_accessed=16 * MIB),
        name="local_part",
    )(in_hbm(feats), residual, short_taps, filter_taps, skip)


def head_kernel(start, carry_ref, first_ref, res_ref, short_ref, skip_ref, toep_ref, gate_ref, q_ref, before_ref, stream_ref, ss_ref):
    per_tile = toep_ref.shape[1] // HEAD
    rows = 2 * HEAD
    row = lax.broadcasted_iota(jnp.int32, (16, LANES), 0)
    total = before_ref[-rows:] if before_ref.shape[0] >= rows else jnp.zeros((rows, LANES), F32)
    for c in range(carry_ref.shape[1] // LANES):
        near = slice(c * LANES, (c + 1) * LANES)
        lanes = slice(start + c * LANES, start + (c + 1) * LANES)
        rim = carry_ref[LANES:, near].astype(F32)
        carry = carry_ref[:LANES, near]
        feats = []
        for s in range(3):
            x = first_ref[s, :, lanes].astype(F32)
            w = [short_ref[i, s : s + 1, lanes] for i in range(3)]
            older, newer = rim[2 * s : 2 * s + 1], rim[2 * s + 1 : 2 * s + 2]
            x1 = jnp.where(row == 0, newer, pltpu.roll(x, 1, 0))
            x2 = jnp.where(row == 0, older, jnp.where(row == 1, newer, pltpu.roll(x, 2, 0)))
            feats.append(w[0] * x + w[1] * x1 + w[2] * x2)
        fixed = (rounded(feats[1]) * rounded(feats[2])).astype(BF16)
        gate = jnp.concatenate([fixed, gate_ref[16 : LANES + HEAD, lanes]], 0)
        query = jnp.concatenate([feats[0].astype(BF16), q_ref[16:rows, lanes]], 0)
        rhs = jnp.concatenate(
            [jnp.concatenate([carry, gate[:LANES]], 0), jnp.concatenate([carry[HEAD:], gate], 0)], 1
        )
        prod = jnp.dot(toep_ref[start // LANES + c], rhs, preferred_element_type=F32)
        filtered = group_select(prod, per_tile, HEAD)
        filtered = filtered + skip_ref[:, lanes] * gate[:rows].astype(F32)
        stream = (res_ref[:rows, lanes].astype(F32) + query.astype(F32) * filtered).astype(BF16)
        stream_ref[:, near] = stream
        wide_stream = stream.astype(F32)
        total = total + wide_stream * wide_stream
    if ss_ref.shape[0] == 8:
        total = jnp.concatenate([total, before_ref[: 2 * TAIL]], 0)
        sums = jnp.sum(jnp.transpose(total), axis=0, keepdims=True)
        ss_ref[...] = jnp.broadcast_to(sums, ss_ref.shape)
    else:
        ss_ref[: 2 * TAIL] = before_ref[: 2 * TAIL]
        ss_ref[2 * TAIL :] = total


def head_part(start, last, carry, first, residual, short_taps, skip, toep, gate, query, before):
    tokens = residual.shape[0]
    ss_shape = (8, tokens) if last else (tokens, LANES)
    return pl.pallas_call(
        functools.partial(head_kernel, start),
        in_specs=[VMEM] * 9,
        out_specs=[VMEM] * 2,
        out_shape=[
            jax.ShapeDtypeStruct((2 * HEAD, carry.shape[1]), BF16),
            jax.ShapeDtypeStruct(ss_shape, F32),
        ],
        compiler_params=pltpu.CompilerParams(vmem_limit_bytes=8 * MIB),
        name="head_part",
    )(carry, first, residual, short_taps, skip, toep, gate, query, before)


def norm_kernel(width, ss_ref, *refs):
    *head_refs, tail_ref, gain_ref, out_ref, buf, sem = refs
    tokens = buf.shape[0]
    split = head_refs[0].shape[0]
    sums = jnp.sum(ss_ref[...], axis=0, keepdims=True)
    scale = jnp.transpose(jnp.broadcast_to(lax.rsqrt(sums / width + EPS), (LANES, tokens)))
    copies = []
    step = tokens // NORM_BLOCKS
    for b in range(NORM_BLOCKS):
        begin, end = b * step, (b + 1) * step
        for low, high, offset, refs_here in (
            (begin, min(end, split), 0, head_refs),
            (max(begin, split), end, split, [tail_ref]),
        ):
            if high <= low:
                continue
            base = 0
            for ref in refs_here:
                for t in range(ref.shape[1] // LANES):
                    near = slice(t * LANES, (t + 1) * LANES)
                    lanes = slice(base + t * LANES, base + (t + 1) * LANES)
                    value = ref[low - offset : high - offset, near].astype(F32)
                    buf[low:high, lanes] = (value * scale[low:high] * gain_ref[:, lanes]).astype(BF16)
                base += ref.shape[1]
        copy = pltpu.make_async_copy(buf.at[begin:end], out_ref.at[begin:end], sem.at[b])
        copy.start()
        copies.append(copy)
    for copy in copies:
        copy.wait()


def normalize(ss, heads, tail, gain, width):
    tokens = heads[0].shape[0] + tail.shape[0]
    channels = tail.shape[1]
    return pl.pallas_call(
        functools.partial(norm_kernel, width),
        in_specs=[VMEM] * (3 + len(heads)),
        out_specs=pl.BlockSpec(memory_space=pl.ANY),
        out_shape=jax.ShapeDtypeStruct((tokens, channels), BF16),
        scratch_shapes=[pltpu.VMEM((tokens, channels), BF16), pltpu.SemaphoreType.DMA((NORM_BLOCKS,))],
        compiler_params=pltpu.CompilerParams(vmem_limit_bytes=8 * MIB),
        name="normalize",
    )(ss, *heads, tail, gain)


def on_device(residual, features, short_taps, filter_taps, skip_gain, norm_gain):
    channels = residual.shape[1]
    feats = jnp.transpose(features, (1, 0, 2))
    skip = skip_gain.reshape(1, channels)
    gain = norm_gain.reshape(1, channels)
    size = lax.axis_size("ctx")
    route = [(i, i + 1) for i in range(size - 1)]
    starts = [sum(WIDTHS[:i]) for i in range(len(WIDTHS))]
    parts = [tail_gate(feats, short_taps, s, w) for s, w in zip(starts, WIDTHS)]
    cut = size // 2 - 1
    early = [pair for pair in route if pair != (cut - 1, cut)]
    carries = [lax.ppermute(part, "ctx", route if i else early) for i, part in enumerate(parts)]
    carries[0] = carries[0] + lax.ppermute(parts[0], "ctx", [(cut - 1, cut)])
    toep, gate, query, first, tail, ss = local_part(feats, residual, short_taps, filter_taps, skip)
    heads = []
    for start, carry in zip(starts, carries):
        last = start + carry.shape[1] == channels
        head, ss = head_part(start, last, carry, first, residual, short_taps, skip, toep, gate, query, ss)
        heads.append(head)
    ss = lax.all_gather(ss[0], "tp")
    return normalize(ss, heads, tail, gain, channels * lax.axis_size("tp"))


def solution(mesh):
    in_specs = (
        P("ctx", "tp"),
        P("ctx", None, "tp"),
        P(None, None, "tp"),
        P("tp", None),
        P("tp"),
        P("tp"),
    )
    return jax.shard_map(
        on_device, mesh=mesh, in_specs=in_specs, out_specs=P("ctx", "tp"), check_vma=False
    )
```

```python
import functools

import jax
import jax.numpy as jnp
from jax import lax
from jax.experimental import pallas as pl
from jax.experimental.pallas import tpu as pltpu
from jax.sharding import PartitionSpec as P

F32 = jnp.float32
BF16 = jnp.bfloat16
LANES = 128
HEAD = 80
TAIL = 48
EPS = 1e-06
WIDTHS = (1152, 640, 256)
UNROLL = 2
NORM_BLOCKS = 8
VMEM = pl.BlockSpec(memory_space=pltpu.VMEM)
MIB = 1 << 20


def in_hbm(x):
    return pltpu.with_memory_space_constraint(x, pltpu.HBM)


def rounded(x):
    return x.astype(BF16).astype(F32)


def causal3(x, w):
    return w[0] * x + w[1] * pltpu.roll(x, 1, 0) + w[2] * pltpu.roll(x, 2, 0)


def gate_tile(load_kv, last_q, taps, halo):
    raw = [load_kv(s).astype(F32) for s in range(2)]
    feat = [causal3(raw[s], taps[s])[halo:] for s in range(2)]
    gate = (rounded(feat[0]) * rounded(feat[1])).astype(BF16)
    last_q = pltpu.roll(last_q.astype(F32)[-8:], 2, 0)
    last_k = pltpu.roll(raw[0][-8:], 4, 0)
    last_v = pltpu.roll(raw[1][-8:], 6, 0)
    row = lax.broadcasted_iota(jnp.int32, last_q.shape, 0)
    rim = jnp.where(row < 2, last_q, jnp.where(row < 4, last_k, jnp.where(row < 6, last_v, 0.0)))
    return gate, rim.astype(BF16)


def tail_gate_kernel(begin, feats_ref, short_ref, out_ref, kv_ref, q_ref, taps_ref, sem):
    rows = feats_ref.shape[1]
    width = out_ref.shape[1]
    halo = kv_ref.shape[1] - LANES
    here = pl.ds(begin, width)
    copies = [
        pltpu.make_async_copy(feats_ref.at[pl.ds(1, 2), pl.ds(rows - LANES - halo, LANES + halo), here], kv_ref, sem.at[0]),
        pltpu.make_async_copy(feats_ref.at[0, pl.ds(rows - 16, 16), here], q_ref, sem.at[1]),
        pltpu.make_async_copy(short_ref.at[:, :, here], taps_ref, sem.at[2]),
    ]
    for copy in copies:
        copy.start()
    for copy in copies:
        copy.wait()
    for t in range(width // LANES):
        lanes = slice(t * LANES, (t + 1) * LANES)
        taps = [[taps_ref[i, s : s + 1, lanes] for i in range(3)] for s in (1, 2)]
        gate, rim = gate_tile(lambda s: kv_ref[s, :, lanes], q_ref[:, lanes], taps, halo)
        out_ref[:LANES, lanes] = gate
        out_ref[LANES:, lanes] = rim


def tail_gate(feats, short_taps, begin, width):
    halo = 8
    return pl.pallas_call(
        functools.partial(tail_gate_kernel, begin),
        in_specs=[pl.BlockSpec(memory_space=pltpu.HBM)] * 2,
        out_specs=VMEM,
        out_shape=jax.ShapeDtypeStruct((LANES + 8, width), BF16),
        scratch_shapes=[
            pltpu.VMEM((2, LANES + halo, width), BF16),
            pltpu.VMEM((16, width), BF16),
            pltpu.VMEM((3, 3, width), F32),
            pltpu.SemaphoreType.DMA((3,)),
        ],
        compiler_params=pltpu.CompilerParams(vmem_limit_bytes=4 * MIB),
        name="tail_gate",
    )(in_hbm(feats), in_hbm(short_taps))


def group_select(prod, per_tile, rows):
    lane = lax.broadcasted_iota(jnp.int32, (rows, 2 * LANES), 1)
    owner = (lane % LANES) // (LANES // per_tile)
    acc = prod[:rows]
    for g in range(1, per_tile):
        acc = jnp.where(owner == g, prod[g * rows : (g + 1) * rows], acc)
    return jnp.concatenate([acc[:, :LANES], acc[:, LANES:]], 0)


def local_kernel(
    hbm_ref, res_ref, short_ref, filt_ref, skip_ref, toep_ref, gate_ref, q_ref, first_ref, stream_ref, ss_ref, feats_ref, sem
):
    tokens, channels = res_ref.shape
    part = UNROLL * LANES

    def load(p):
        lanes = pl.ds(pl.multiple_of(p * part, part), part)
        return pltpu.make_async_copy(hbm_ref.at[:, :, lanes], feats_ref.at[:, :, lanes], sem.at[p])

    for p in range(channels // part):
        load(p).start()
    tiles = channels // LANES
    per_tile = filt_ref.shape[0] // tiles
    first = tokens - 2 * TAIL
    tap = lax.broadcasted_iota(jnp.int32, (LANES, 2 * LANES), 0)
    pos = lax.broadcasted_iota(jnp.int32, (LANES, 2 * LANES), 1)
    flip = (tap + pos == LANES).astype(BF16)

    def tile(t):
        lanes = pl.ds(pl.multiple_of(t * LANES, LANES), LANES)
        first_ref[:, :, lanes] = feats_ref[:, : first_ref.shape[1], lanes]
        feats = [
            causal3(feats_ref[s, :, lanes].astype(F32), [short_ref[i, s : s + 1, lanes] for i in range(3)])
            for s in range(3)
        ]
        gate = (rounded(feats[1]) * rounded(feats[2])).astype(BF16)
        query = feats[0].astype(BF16)
        gate_ref[:, lanes] = gate
        q_ref[:, lanes] = query
        taps = filt_ref[pl.ds(pl.multiple_of(t * per_tile, per_tile), per_tile), :]
        base = jnp.dot(taps, flip, preferred_element_type=F32)
        lhs = []
        for g in range(per_tile):
            wide = jnp.broadcast_to(base[g : g + 1], (HEAD, 2 * LANES))
            band = pltpu.roll(wide, 0, 1, stride=1, stride_axis=0).astype(BF16)
            toep_ref[t, g * HEAD : (g + 1) * HEAD, :] = band
            lhs.append(band[:TAIL])
        z0 = jnp.zeros((first - LANES, LANES), BF16)
        z1 = jnp.zeros((first - LANES + TAIL, LANES), BF16)
        rhs = jnp.concatenate(
            [
                jnp.concatenate([gate[first - LANES :], z0], 0),
                jnp.concatenate([gate[first - LANES + TAIL :], z1], 0),
            ],
            1,
        )
        prod = jnp.dot(jnp.concatenate(lhs, 0), rhs, preferred_element_type=F32)
        filtered = group_select(prod, per_tile, TAIL)
        filtered = filtered + skip_ref[:, lanes] * gate[first:].astype(F32)
        stream = (res_ref[first:, lanes].astype(F32) + query[first:].astype(F32) * filtered).astype(BF16)
        stream_ref[:, lanes] = stream
        wide_stream = stream.astype(F32)
        return wide_stream * wide_stream

    def step(p, total):
        load(p).wait()
        for u in range(UNROLL):
            total = total + tile(p * UNROLL + u)
        return total

    ss_ref[...] = lax.fori_loop(0, tiles // UNROLL, step, jnp.zeros((2 * TAIL, LANES), F32))


def local_part(feats, residual, short_taps, filter_taps, skip):
    _, tokens, channels = feats.shape
    tiles = channels // LANES
    per_tile = filter_taps.shape[0] // tiles
    return pl.pallas_call(
        local_kernel,
        in_specs=[pl.BlockSpec(memory_space=pltpu.HBM)] + [VMEM] * 4,
        out_specs=[VMEM] * 6,
        out_shape=[
            jax.ShapeDtypeStruct((tiles, per_tile * HEAD, 2 * LANES), BF16),
            jax.ShapeDtypeStruct((tokens, channels), BF16),
            jax.ShapeDtypeStruct((tokens, channels), BF16),
            jax.ShapeDtypeStruct((3, 16, channels), BF16),
            jax.ShapeDtypeStruct((2 * TAIL, channels), BF16),
            jax.ShapeDtypeStruct((2 * TAIL, LANES), F32),
        ],
        scratch_shapes=[
            pltpu.VMEM(feats.shape, BF16),
            pltpu.SemaphoreType.DMA((channels // (UNROLL * LANES),)),
        ],
        compiler_params=pltpu.CompilerParams(vmem_limit_bytes=16 * MIB),
        cost_estimate=pl.CostEstimate(flops=10**9, transcendentals=0, bytes_accessed=16 * MIB),
        name="local_part",
    )(in_hbm(feats), residual, short_taps, filter_taps, skip)


def head_kernel(start, carry_ref, first_ref, res_ref, short_ref, skip_ref, toep_ref, gate_ref, q_ref, before_ref, stream_ref, ss_ref):
    per_tile = toep_ref.shape[1] // HEAD
    rows = 2 * HEAD
    row = lax.broadcasted_iota(jnp.int32, (16, LANES), 0)
    total = before_ref[-rows:] if before_ref.shape[0] >= rows else jnp.zeros((rows, LANES), F32)
    for c in range(carry_ref.shape[1] // LANES):
        near = slice(c * LANES, (c + 1) * LANES)
        lanes = slice(start + c * LANES, start + (c + 1) * LANES)
        rim = carry_ref[LANES:, near].astype(F32)
        carry = carry_ref[:LANES, near]
        feats = []
        for s in range(3):
            x = first_ref[s, :, lanes].astype(F32)
            w = [short_ref[i, s : s + 1, lanes] for i in range(3)]
            older, newer = rim[2 * s : 2 * s + 1], rim[2 * s + 1 : 2 * s + 2]
            x1 = jnp.where(row == 0, newer, pltpu.roll(x, 1, 0))
            x2 = jnp.where(row == 0, older, jnp.where(row == 1, newer, pltpu.roll(x, 2, 0)))
            feats.append(w[0] * x + w[1] * x1 + w[2] * x2)
        fixed = (rounded(feats[1]) * rounded(feats[2])).astype(BF16)
        gate = jnp.concatenate([fixed, gate_ref[16 : LANES + HEAD, lanes]], 0)
        query = jnp.concatenate([feats[0].astype(BF16), q_ref[16:rows, lanes]], 0)
        rhs = jnp.concatenate(
            [jnp.concatenate([carry, gate[:LANES]], 0), jnp.concatenate([carry[HEAD:], gate], 0)], 1
        )
        prod = jnp.dot(toep_ref[start // LANES + c], rhs, preferred_element_type=F32)
        filtered = group_select(prod, per_tile, HEAD)
        filtered = filtered + skip_ref[:, lanes] * gate[:rows].astype(F32)
        stream = (res_ref[:rows, lanes].astype(F32) + query.astype(F32) * filtered).astype(BF16)
        stream_ref[:, near] = stream
        wide_stream = stream.astype(F32)
        total = total + wide_stream * wide_stream
    if ss_ref.shape[0] == 8:
        total = jnp.concatenate([total, before_ref[: 2 * TAIL]], 0)
        sums = jnp.sum(jnp.transpose(total), axis=0, keepdims=True)
        ss_ref[...] = jnp.broadcast_to(sums, ss_ref.shape)
    else:
        ss_ref[: 2 * TAIL] = before_ref[: 2 * TAIL]
        ss_ref[2 * TAIL :] = total


def head_part(start, last, carry, first, residual, short_taps, skip, toep, gate, query, before):
    tokens = residual.shape[0]
    ss_shape = (8, tokens) if last else (tokens, LANES)
    return pl.pallas_call(
        functools.partial(head_kernel, start),
        in_specs=[VMEM] * 9,
        out_specs=[VMEM] * 2,
        out_shape=[
            jax.ShapeDtypeStruct((2 * HEAD, carry.shape[1]), BF16),
            jax.ShapeDtypeStruct(ss_shape, F32),
        ],
        compiler_params=pltpu.CompilerParams(vmem_limit_bytes=8 * MIB),
        name="head_part",
    )(carry, first, residual, short_taps, skip, toep, gate, query, before)


def norm_kernel(width, ss_ref, *refs):
    *head_refs, tail_ref, gain_ref, out_ref, buf, sem = refs
    tokens = buf.shape[0]
    split = head_refs[0].shape[0]
    sums = jnp.sum(ss_ref[...], axis=0, keepdims=True)
    scale = jnp.transpose(jnp.broadcast_to(lax.rsqrt(sums / width + EPS), (LANES, tokens)))
    copies = []
    step = tokens // NORM_BLOCKS
    for b in range(NORM_BLOCKS):
        begin, end = b * step, (b + 1) * step
        for low, high, offset, refs_here in (
            (begin, min(end, split), 0, head_refs),
            (max(begin, split), end, split, [tail_ref]),
        ):
            if high <= low:
                continue
            base = 0
            for ref in refs_here:
                for t in range(ref.shape[1] // LANES):
                    near = slice(t * LANES, (t + 1) * LANES)
                    lanes = slice(base + t * LANES, base + (t + 1) * LANES)
                    value = ref[low - offset : high - offset, near].astype(F32)
                    buf[low:high, lanes] = (value * scale[low:high] * gain_ref[:, lanes]).astype(BF16)
                base += ref.shape[1]
        copy = pltpu.make_async_copy(buf.at[begin:end], out_ref.at[begin:end], sem.at[b])
        copy.start()
        copies.append(copy)
    for copy in copies:
        copy.wait()


def normalize(ss, heads, tail, gain, width):
    tokens = heads[0].shape[0] + tail.shape[0]
    channels = tail.shape[1]
    return pl.pallas_call(
        functools.partial(norm_kernel, width),
        in_specs=[VMEM] * (3 + len(heads)),
        out_specs=pl.BlockSpec(memory_space=pl.ANY),
        out_shape=jax.ShapeDtypeStruct((tokens, channels), BF16),
        scratch_shapes=[pltpu.VMEM((tokens, channels), BF16), pltpu.SemaphoreType.DMA((NORM_BLOCKS,))],
        compiler_params=pltpu.CompilerParams(vmem_limit_bytes=8 * MIB),
        name="normalize",
    )(ss, *heads, tail, gain)


def on_device(residual, features, short_taps, filter_taps, skip_gain, norm_gain):
    channels = residual.shape[1]
    feats = jnp.transpose(features, (1, 0, 2))
    skip = skip_gain.reshape(1, channels)
    gain = norm_gain.reshape(1, channels)
    size = lax.axis_size("ctx")
    route = [(i, i + 1) for i in range(size - 1)]
    starts = [sum(WIDTHS[:i]) for i in range(len(WIDTHS))]
    parts = [tail_gate(feats, short_taps, s, w) for s, w in zip(starts, WIDTHS)]
    cut = size // 2 - 1
    early = [pair for pair in route if pair != (cut - 1, cut)]
    carries = [lax.ppermute(part, "ctx", route if i else early) for i, part in enumerate(parts)]
    carries[0] = carries[0] + lax.ppermute(parts[0], "ctx", [(cut - 1, cut)])
    toep, gate, query, first, tail, ss = local_part(feats, residual, short_taps, filter_taps, skip)
    heads = []
    for start, carry in zip(starts, carries):
        last = start + carry.shape[1] == channels
        head, ss = head_part(start, last, carry, first, residual, short_taps, skip, toep, gate, query, ss)
        heads.append(head)
    ss = lax.all_gather(ss[0], "tp")
    return normalize(ss, heads, tail, gain, channels * lax.axis_size("tp"))


def solution(mesh):
    in_specs = (
        P("ctx", "tp"),
        P("ctx", None, "tp"),
        P(None, None, "tp"),
        P("tp", None),
        P("tp"),
        P("tp"),
    )
    return jax.shard_map(
        on_device, mesh=mesh, in_specs=in_specs, out_specs=P("ctx", "tp"), check_vma=False
    )
```
